32 devices in a mesh: shot: 2 (over x), strip: 16 (over z, y, core).
Axes of the slice: x: 2, y: 2, z: 4, core: 2. Of those that a mesh axis runs over, the one named last changes fastest.
Arguments:
- waves: float32 [2, 2, 8, 512, 512], P(None, None, 'shot', 'strip'), parts along dimension 2, may hold values from -6 to 6
- levels: int32 [512, 512], P('strip'), may hold values from 0 to 4
- coeffs: float32 [2, 4, 5, 17], replicated, may hold values from -0.7 to 0.7
- angles: float32 [4, 5], replicated, may hold values from -3.140625 to 3.140625
- order: int32 [8], P('shot'), parts along dimension 0, may hold values from 0 to 3, each once
Outputs:
- waves_out: float32 [2, 2, 8, 512, 512], P(None, None, 'shot', 'strip'), parts along dimension 2
- image: float32 [4, 512, 512], P('shot', 'strip'), parts along dimension 0
The draws below stay inside these ranges and needn't reach their ends.
There are 2 independent parts, one for each index of `shot`. The reference program is written for one: setup_inputs(seed, part) draws one part's arguments, and reference() takes and returns one part's arrays. A program takes and returns all parts, laid end to end along the dimension named above; an argument that names none is the same for every part. Nothing has to cross between parts.
Inputs may be any that keep to these rules, and one draw needn't show every extreme that they name: order names every table row once.
All inputs are finite; a program needn't handle non-finite values.
Results may differ from the reference program's by a relative error of at most 0.00013.
Values sent between devices are 32-bit elements; how exact they have to be, the bound alone decides.
A program may use at most 64 MiB of HBM per device.

```python
import jax
import jax.numpy as jnp
from jax import lax

INLINE = 512
FREQ = 4
LEVELS = 5
TAPS = 17
STEPS = 2
CROSS = 512


def set_ends(array, key, least, top_value):
    longest = array.shape.index(max(array.shape))
    spots = []
    for shift in (0, 1):
        where = [jax.random.randint(jax.random.fold_in(key, axis), (), 0, length) for axis, length in enumerate(array.shape)]
        where[longest] = (where[longest] + shift) % array.shape[longest]
        spots.append(tuple(where))
    return array.at[spots[0]].set(least).at[spots[1]].set(top_value)


def steps_of(rng, dims, split, smallest, high):
    factor_of = 1.0
    for position, shards_of in split:
        heights = jax.random.uniform(jax.random.fold_in(jax.random.fold_in(rng, 6), position), (shards_of,), jnp.float32, smallest / len(split), high / len(split))
        factor_of = factor_of * jnp.repeat(jnp.exp(heights), dims[position] // shards_of).reshape((-1,) + (1,) * (len(dims) - 1 - position))
    return factor_of


def gaussian(rng, shape, scale, most, split=(), kind=jnp.bfloat16):
    entries = scale * jax.random.normal(rng, shape, jnp.float32)
    if split:
        entries = entries * steps_of(rng, shape, split, -0.22, 0.18)
    return jnp.clip(entries, -most, most).astype(kind)


def setup_inputs(seed: int = 0, part: int = 0) -> dict:
    key_of = jax.random.split(jax.random.key(seed), 6)
    part_keys = jax.random.split(jax.random.fold_in(key_of[5], part), 6)
    waves = gaussian(part_keys[0], (2, 2, FREQ, CROSS, INLINE), 1.0, 6.0, ((3, 16),), jnp.float32)
    levels = set_ends(jax.random.randint(key_of[1], (CROSS, INLINE), 0, LEVELS), jax.random.fold_in(key_of[1], 1), 0, LEVELS - 1).astype(jnp.int32)
    coeffs = gaussian(key_of[2], (2, FREQ, LEVELS, TAPS), 0.17, 0.7, (), jnp.float32)
    angles = jnp.clip(jax.random.uniform(key_of[3], (FREQ, LEVELS), jnp.float32, -3.140625, 3.140625), -3.140625, 3.140625)
    order = jax.random.permutation(part_keys[4], FREQ).astype(jnp.int32)
    return {"waves": waves, "levels": levels, "coeffs": coeffs, "angles": angles, "order": order}


def one_pass(field_real, field_imag, coef_table, levels, along_axis, conj_sign, half_taps):
    widths = [(0, 0), (0, 0), (0, 0)]
    widths[along_axis] = (half_taps, half_taps)
    pad_real = jnp.pad(field_real, widths)
    pad_imag = jnp.pad(field_imag, widths)
    out_length = field_real.shape[along_axis]
    acc_real = jnp.zeros(field_real.shape, jnp.float32)
    acc_imag = jnp.zeros(field_real.shape, jnp.float32)
    for tap_index in range(2 * half_taps + 1):
        shift_real = lax.slice_in_dim(pad_real, tap_index, tap_index + out_length, axis=along_axis)
        shift_imag = lax.slice_in_dim(pad_imag, tap_index, tap_index + out_length, axis=along_axis)
        coef_real = coef_table[0][:, levels, tap_index]
        coef_imag = coef_table[1][:, levels, tap_index] * conj_sign
        acc_real = acc_real + (coef_real * shift_real - coef_imag * shift_imag)
        acc_imag = acc_imag + (coef_real * shift_imag + coef_imag * shift_real)
    return acc_real, acc_imag


def reference(waves, levels, coeffs, angles, order):
    coef_table = coeffs[:, order]
    turn_table = angles[order]
    phase_angle = turn_table[:, levels]
    cosine = jnp.cos(phase_angle)
    sine_part = jnp.sin(phase_angle)
    half_taps = (coeffs.shape[3] - 1) // 2
    source_real, source_imag = waves[0, 0], waves[0, 1]
    receiver_real, receiver_imag = waves[1, 0], waves[1, 1]
    slabs = []
    for depth_step in range(STEPS):
        source_real, source_imag = (source_real * cosine - source_imag * sine_part,
                                    source_real * sine_part + source_imag * cosine)
        receiver_real, receiver_imag = (receiver_real * cosine + receiver_imag * sine_part,
                                        -receiver_real * sine_part + receiver_imag * cosine)
        for along_axis in (2, 1):
            source_real, source_imag = one_pass(source_real, source_imag, coef_table, levels, along_axis, 1.0, half_taps)
            receiver_real, receiver_imag = one_pass(receiver_real, receiver_imag, coef_table, levels, along_axis, -1.0, half_taps)
        slabs.append(jnp.sum(source_real * receiver_real + source_imag * receiver_imag, axis=0))
    waves_out = jnp.stack([jnp.stack([source_real, source_imag]), jnp.stack([receiver_real, receiver_imag])])
    return waves_out, jnp.stack(slabs)
```

```python
import functools

import jax
import jax.numpy as jnp
from jax import lax
from jax.experimental import pallas as pl
from jax.experimental.pallas import tpu as pltpu
from jax.sharding import PartitionSpec as P

STEPS = 2
LANES = 128
SUBS = 8
PAIR = 2
MESH = pl.DeviceIdType.MESH


def tile_rows(index, count=1):
    return pl.ds(pl.multiple_of(index * SUBS, SUBS), count * SUBS)


def kernel(
    sizes, waves_ref, levels_ref, coeffs_ref, angles_ref, order_ref, out_ref, image_ref,
    level_buf, coef_buf, turn_buf, field_buf, mid_buf, image_buf, send_sem, recv_sem,
):
    freqs, rows, blocks, per_tile, groups, levels, taps, strips = sizes
    half = taps // 2
    span = rows + 2 * half
    me = lax.axis_index("strip")
    has_low, has_high = me > 0, me < strips - 1

    def neighbour(step):
        return {"strip": me + step}

    barrier = pltpu.get_barrier_semaphore()
    for there, step in ((has_low, -1), (has_high, 1)):

        @pl.when(there)
        def _():
            pl.semaphore_signal(barrier, inc=1, device_id=neighbour(step), device_id_type=MESH)

    lane = lax.broadcasted_iota(jnp.int32, (SUBS, LANES), 1)
    sub = lax.broadcasted_iota(jnp.int32, (SUBS, LANES), 0)
    block_of = lax.rem(sub, blocks)

    for top in range(0, rows, SUBS):
        for block in range(blocks):
            cells = levels_ref[top : top + SUBS, block * LANES : (block + 1) * LANES]
            for member in range(per_tile):
                level_buf[pl.ds(top * SUBS + member * blocks + block, SUBS, stride=SUBS), :] = cells

    def by_member(values):
        tile = jnp.full((SUBS, LANES), values[0], jnp.float32)
        for member in range(1, per_tile):
            tile = jnp.where(sub >= member * blocks, values[member], tile)
        return tile

    slots = [order_ref[f] for f in range(freqs)]
    coef_tabs, cos_tabs, sin_tabs = [], [], []
    for group in range(groups):
        members = slots[group * per_tile : (group + 1) * per_tile]
        tabs = [jnp.zeros((SUBS, LANES), jnp.float32) for _ in range(2)]
        turn = jnp.zeros((SUBS, LANES), jnp.float32)
        for level in range(levels):
            for tap in range(taps):
                hit = lane == tap * levels + level
                for part in range(2):
                    entry = by_member([coeffs_ref[part, row, level, tap] for row in members])
                    tabs[part] = jnp.where(hit, entry, tabs[part])
            turn = jnp.where(lane == level, by_member([angles_ref[row, level] for row in members]), turn)
        coef_tabs.append(tabs)
        cos_tabs.append(jnp.cos(turn))
        sin_tabs.append(jnp.sin(turn))

    def pick(table, index):
        return jnp.take_along_axis(table, index, axis=1)

    def coef_at(group, y, tap, part):
        return tile_rows(((group * rows + y) * taps + tap) * 2 + part)

    def turn_at(group, y, which):
        return tile_rows((group * rows + y) * 2 + which)

    @pl.loop(0, rows)
    def _(y):
        level_tile = level_buf[tile_rows(y), :]
        for group in range(groups):
            turn_buf[turn_at(group, y, 0), :] = pick(cos_tabs[group], level_tile)
            turn_buf[turn_at(group, y, 1), :] = pick(sin_tabs[group], level_tile)
        for tap in range(taps):
            index = level_tile + tap * levels
            for group in range(groups):
                for part in range(2):
                    coef_buf[coef_at(group, y, tap, part), :] = pick(coef_tabs[group][part], index)

    def field_at(group, comp, y):
        return tile_rows((group * 4 + comp) * rows + y)

    def mid_at(step, group, y, comp):
        return tile_rows(((step * groups + group) * span + y) * 4 + comp)

    for group in range(groups):
        for comp in range(4):
            for member in range(per_tile):
                for top in range(0, rows, SUBS):
                    for block in range(blocks):
                        cells = waves_ref[
                            comp // 2, comp % 2, group * per_tile + member, top : top + SUBS,
                            block * LANES : (block + 1) * LANES,
                        ]
                        start = ((group * 4 + comp) * rows + top) * SUBS + member * blocks + block
                        field_buf[pl.ds(start, SUBS, stride=SUBS), :] = cells

    for there, first in ((has_low, 0), (has_high, rows + half)):

        @pl.when(jnp.logical_not(there))
        def _():
            for step in range(STEPS):
                for group in range(groups):

                    @pl.loop(0, half * 4)
                    def _(i):
                        mid_buf[tile_rows(((step * groups + group) * span + first) * 4 + i), :] = jnp.zeros(
                            (SUBS, LANES), jnp.float32
                        )

    pl.semaphore_wait(barrier, has_low.astype(jnp.int32) + has_high.astype(jnp.int32))

    def halo_copy(step, group, side):
        source, target = ((half, rows + half), (rows, 0))[side]
        base = (step * groups + group) * span
        return pltpu.make_async_remote_copy(
            src_ref=mid_buf.at[tile_rows((base + source) * 4, half * 4)],
            dst_ref=mid_buf.at[tile_rows((base + target) * 4, half * 4)],
            send_sem=send_sem.at[step, group, side],
            recv_sem=recv_sem.at[step, group, side],
            device_id=neighbour((-1, 1)[side]),
            device_id_type=MESH,
        )

    def inline_row(step, group, y):
        cosine = turn_buf[turn_at(group, y, 0), :]
        sine = turn_buf[turn_at(group, y, 1), :]
        sr, si, rr, ri = [field_buf[field_at(group, comp, y), :] for comp in range(4)]
        cells = (sr * cosine - si * sine, sr * sine + si * cosine, rr * cosine + ri * sine, ri * cosine - rr * sine)
        before = [jnp.where(block_of == 0, 0.0, pltpu.roll(v, 1, 0)) for v in cells]
        after = [jnp.where(block_of == blocks - 1, 0.0, pltpu.roll(v, SUBS - 1, 0)) for v in cells]
        acc = [None] * 4
        for tap in range(taps):
            shift = tap - half
            if shift < 0:
                moved = [
                    pltpu.roll(jnp.where(lane < LANES + shift, v, w), -shift, 1) for v, w in zip(cells, before)
                ]
            elif shift > 0:
                moved = [
                    pltpu.roll(jnp.where(lane >= shift, v, w), LANES - shift, 1) for v, w in zip(cells, after)
                ]
            else:
                moved = cells
            add_tap(acc, group, y, tap, moved)
        for comp in range(4):
            mid_buf[mid_at(step, group, y + half, comp), :] = acc[comp]

    def add_tap(acc, group, y, tap, moved):
        cr = coef_buf[coef_at(group, y, tap, 0), :]
        ci = coef_buf[coef_at(group, y, tap, 1), :]
        sr, si, rr, ri = moved
        if acc[0] is None:
            acc[:] = [cr * sr - ci * si, cr * si + ci * sr, cr * rr + ci * ri, cr * ri - ci * rr]
        else:
            acc[0] = acc[0] + cr * sr - ci * si
            acc[1] = acc[1] + cr * si + ci * sr
            acc[2] = acc[2] + cr * rr + ci * ri
            acc[3] = acc[3] + cr * ri - ci * rr

    def inline_pass(step, group):
        @pl.loop(0, half)
        def _(y):
            inline_row(step, group, y)

        @pl.loop(rows - half, rows)
        def _(y):
            inline_row(step, group, y)

        for side, there in enumerate((has_low, has_high)):

            @pl.when(there)
            def _():
                halo_copy(step, group, side).start()

        @pl.loop(half, rows - half)
        def _(y):
            inline_row(step, group, y)

    def cross_pass(step, group):
        for side, there in ((1, has_low), (0, has_high)):

            @pl.when(there)
            def _():
                halo_copy(step, group, side).wait_recv()

        @pl.loop(0, rows // PAIR)
        def _(trip):
            y = trip * PAIR
            accs = [[None] * 4 for _ in range(PAIR)]
            for line in range(taps + PAIR - 1):
                moved = [mid_buf[mid_at(step, group, y + line, comp), :] for comp in range(4)]
                for place in range(PAIR):
                    if 0 <= line - place < taps:
                        add_tap(accs[place], group, y + place, line - place, moved)
            for place, acc in enumerate(accs):
                for comp in range(4):
                    field_buf[field_at(group, comp, y + place), :] = acc[comp]
                term = acc[0] * acc[2] + acc[1] * acc[3]
                at = tile_rows(step * rows + y + place)
                if group == 0:
                    image_buf[at, :] = term
                else:
                    image_buf[at, :] = image_buf[at, :] + term

    for step in range(STEPS):
        for group in range(groups):
            inline_pass(step, group)
        for group in range(groups):
            cross_pass(step, group)

    for group in range(groups):
        for comp in range(4):
            for member in range(per_tile):
                for top in range(0, rows, SUBS):
                    for block in range(blocks):
                        start = ((group * 4 + comp) * rows + top) * SUBS + member * blocks + block
                        out_ref[
                            comp // 2, comp % 2, group * per_tile + member, top : top + SUBS,
                            block * LANES : (block + 1) * LANES,
                        ] = field_buf[pl.ds(start, SUBS, stride=SUBS), :]
    for step in range(STEPS):
        for top in range(0, rows, SUBS):
            for block in range(blocks):
                total = None
                for member in range(per_tile):
                    start = (step * rows + top) * SUBS + member * blocks + block
                    term = image_buf[pl.ds(start, SUBS, stride=SUBS), :]
                    total = term if total is None else total + term
                image_ref[step, top : top + SUBS, block * LANES : (block + 1) * LANES] = total

    for step in range(STEPS):
        for group in range(groups):
            for side, there in enumerate((has_low, has_high)):

                @pl.when(there)
                def _():
                    halo_copy(step, group, side).wait_send()


def on_device(strips, waves, levels, coeffs, angles, order):
    freqs, rows, cells = waves.shape[2:]
    level_count, taps = coeffs.shape[2:]
    blocks = cells // LANES
    per_tile = SUBS // blocks
    groups = freqs // per_tile
    assert blocks * per_tile == SUBS and groups * per_tile == freqs
    assert rows % SUBS == 0 and rows >= taps - 1 and level_count * taps <= LANES
    half = taps // 2
    sizes = (freqs, rows, blocks, per_tile, groups, level_count, taps, strips)
    tiles = lambda count: pltpu.VMEM((count * SUBS, LANES), jnp.float32)
    vmem, smem = pl.BlockSpec(memory_space=pltpu.VMEM), pl.BlockSpec(memory_space=pltpu.SMEM)
    return pl.pallas_call(
        functools.partial(kernel, sizes),
        out_shape=(
            jax.ShapeDtypeStruct(waves.shape, jnp.float32),
            jax.ShapeDtypeStruct((STEPS, rows, cells), jnp.float32),
        ),
        in_specs=[vmem, vmem, smem, smem, smem],
        out_specs=(vmem, vmem),
        scratch_shapes=[
            pltpu.VMEM((rows * SUBS, LANES), jnp.int32),
            tiles(groups * rows * taps * 2),
            tiles(groups * rows * 2),
            tiles(groups * 4 * rows),
            tiles(STEPS * groups * (rows + 2 * half) * 4),
            tiles(STEPS * rows),
            pltpu.SemaphoreType.DMA((STEPS, groups, 2)),
            pltpu.SemaphoreType.DMA((STEPS, groups, 2)),
        ],
        compiler_params=pltpu.CompilerParams(
            collective_id=0, has_side_effects=True, vmem_limit_bytes=48 * 1024 * 1024
        ),
    )(waves, levels, coeffs, angles, order)


def solution(mesh):
    in_specs = (P(None, None, "shot", "strip", None), P("strip", None), P(), P(), P("shot"))
    out_specs = (P(None, None, "shot", "strip", None), P("shot", "strip", None))
    return jax.shard_map(
        functools.partial(on_device, mesh.shape["strip"]),
        mesh=mesh,
        in_specs=in_specs,
        out_specs=out_specs,
        check_vma=False,
    )
```

```python
import functools

import jax
import jax.numpy as jnp
from jax import lax
from jax.experimental import pallas as pl
from jax.experimental.pallas import tpu as pltpu
from jax.sharding import PartitionSpec as P

STEPS = 2
LANES = 128
SUBS = 8
ROWS = 2
PAIR = 2
MESH = pl.DeviceIdType.MESH


def tile_rows(index, count=1):
    return pl.ds(pl.multiple_of(index * SUBS, SUBS), count * SUBS)


def kernel(
    sizes, waves_ref, levels_ref, coeffs_ref, angles_ref, order_ref, out_ref, image_ref,
    level_buf, table_buf, coef_buf, turn_buf, field_buf, mid_buf, image_buf, send_sem, recv_sem,
):
    freqs, rows, blocks, per_tile, groups, levels, taps, strips = sizes
    half = taps // 2
    span = rows + 2 * half
    me = lax.axis_index("strip")
    has_low, has_high = me > 0, me < strips - 1

    def neighbour(step):
        return {"strip": me + step}

    barrier = pltpu.get_barrier_semaphore()
    for there, step in ((has_low, -1), (has_high, 1)):

        @pl.when(there)
        def _():
            pl.semaphore_signal(barrier, inc=1, device_id=neighbour(step), device_id_type=MESH)

    lane = lax.broadcasted_iota(jnp.int32, (SUBS, LANES), 1)
    sub = lax.broadcasted_iota(jnp.int32, (SUBS, LANES), 0)
    block_of = lax.rem(sub, blocks)

    for top in range(0, rows, SUBS):
        for block in range(blocks):
            cells = levels_ref[top : top + SUBS, block * LANES : (block + 1) * LANES]
            for member in range(per_tile):
                level_buf[pl.ds(top * SUBS + member * blocks + block, SUBS, stride=SUBS), :] = cells

    def table_at(group, tap, part, level):
        return tile_rows(((group * taps + tap) * 2 + part) * levels + level)

    def by_member(values):
        tile = jnp.full((SUBS, LANES), values[0], jnp.float32)
        for member in range(1, per_tile):
            tile = jnp.where(sub >= member * blocks, values[member], tile)
        return tile

    slots = [order_ref[f] for f in range(freqs)]
    turn_tabs = []
    for group in range(groups):
        members = slots[group * per_tile : (group + 1) * per_tile]
        turn = jnp.zeros((SUBS, LANES), jnp.float32)
        for level in range(levels):
            for tap in range(taps):
                for part in range(2):
                    table_buf[table_at(group, tap, part, level), :] = by_member(
                        [coeffs_ref[part, row, level, tap] for row in members]
                    )
            turn = jnp.where(lane == level, by_member([angles_ref[row, level] for row in members]), turn)
        for which, tab in enumerate((jnp.cos(turn), jnp.sin(turn))):
            turn_tabs.append([jnp.broadcast_to(tab[:, level : level + 1], (SUBS, LANES)) for level in range(levels)])

    def coef_at(group, y, tap, part):
        return tile_rows(((group * rows + y) * taps + tap) * 2 + part)

    def turn_at(group, y, which):
        return tile_rows((group * rows + y) * 2 + which)

    def choose(masks, entries):
        tile = entries[0]
        for mask, entry in zip(masks, entries[1:]):
            tile = jnp.where(mask, entry, tile)
        return tile

    @pl.loop(0, rows // PAIR)
    def _(trip):
        y = trip * PAIR
        masks = []
        for place in range(PAIR):
            level_tile = level_buf[tile_rows(y + place), :]
            masks.append([level_tile == level for level in range(1, levels)])
        for group in range(groups):
            for which in range(2):
                for place in range(PAIR):
                    turn_buf[turn_at(group, y + place, which), :] = choose(masks[place], turn_tabs[group * 2 + which])
            for tap in range(taps):
                for part in range(2):
                    entries = [table_buf[table_at(group, tap, part, level), :] for level in range(levels)]
                    for place in range(PAIR):
                        coef_buf[coef_at(group, y + place, tap, part), :] = choose(masks[place], entries)

    def field_at(group, comp, y):
        return tile_rows((group * 4 + comp) * rows + y)

    def mid_at(step, group, y, comp):
        return tile_rows(((step * groups + group) * span + y) * 4 + comp)

    for group in range(groups):
        for comp in range(4):
            for member in range(per_tile):
                for top in range(0, rows, SUBS):
                    for block in range(blocks):
                        cells = waves_ref[
                            comp // 2, comp % 2, group * per_tile + member, top : top + SUBS,
                            block * LANES : (block + 1) * LANES,
                        ]
                        start = ((group * 4 + comp) * rows + top) * SUBS + member * blocks + block
                        field_buf[pl.ds(start, SUBS, stride=SUBS), :] = cells

    for there, first in ((has_low, 0), (has_high, rows + half)):

        @pl.when(jnp.logical_not(there))
        def _():
            for step in range(STEPS):
                for group in range(groups):

                    @pl.loop(0, half * 4)
                    def _(i):
                        mid_buf[tile_rows(((step * groups + group) * span + first) * 4 + i), :] = jnp.zeros(
                            (SUBS, LANES), jnp.float32
                        )

    pl.semaphore_wait(barrier, has_low.astype(jnp.int32) + has_high.astype(jnp.int32))

    def halo_copy(step, group, side):
        source, target = ((half, rows + half), (rows, 0))[side]
        base = (step * groups + group) * span
        return pltpu.make_async_remote_copy(
            src_ref=mid_buf.at[tile_rows((base + source) * 4, half * 4)],
            dst_ref=mid_buf.at[tile_rows((base + target) * 4, half * 4)],
            send_sem=send_sem.at[step, group, side],
            recv_sem=recv_sem.at[step, group, side],
            device_id=neighbour((-1, 1)[side]),
            device_id_type=MESH,
        )

    def inline_row(step, group, y):
        cosine = turn_buf[turn_at(group, y, 0), :]
        sine = turn_buf[turn_at(group, y, 1), :]
        sr, si, rr, ri = [field_buf[field_at(group, comp, y), :] for comp in range(4)]
        cells = (sr * cosine - si * sine, sr * sine + si * cosine, rr * cosine + ri * sine, ri * cosine - rr * sine)
        before = [jnp.where(block_of == 0, 0.0, pltpu.roll(v, 1, 0)) for v in cells]
        after = [jnp.where(block_of == blocks - 1, 0.0, pltpu.roll(v, SUBS - 1, 0)) for v in cells]
        acc = [None] * 4
        for tap in range(taps):
            shift = tap - half
            if shift < 0:
                moved = [
                    pltpu.roll(jnp.where(lane < LANES + shift, v, w), -shift, 1) for v, w in zip(cells, before)
                ]
            elif shift > 0:
                moved = [
                    pltpu.roll(jnp.where(lane >= shift, v, w), LANES - shift, 1) for v, w in zip(cells, after)
                ]
            else:
                moved = cells
            add_tap(acc, group, y, tap, moved)
        for comp in range(4):
            mid_buf[mid_at(step, group, y + half, comp), :] = acc[comp]

    def add_tap(acc, group, y, tap, moved):
        cr = coef_buf[coef_at(group, y, tap, 0), :]
        ci = coef_buf[coef_at(group, y, tap, 1), :]
        sr, si, rr, ri = moved
        if acc[0] is None:
            acc[:] = [cr * sr - ci * si, cr * si + ci * sr, cr * rr + ci * ri, cr * ri - ci * rr]
        else:
            acc[0] = acc[0] + cr * sr - ci * si
            acc[1] = acc[1] + cr * si + ci * sr
            acc[2] = acc[2] + cr * rr + ci * ri
            acc[3] = acc[3] + cr * ri - ci * rr

    def inline_pass(step, group):
        def inline_rows(first, last):
            @pl.loop(first // ROWS, last // ROWS)
            def _(trip):
                for place in range(ROWS):
                    inline_row(step, group, trip * ROWS + place)

        inline_rows(0, half)
        inline_rows(rows - half, rows)

        for side, there in enumerate((has_low, has_high)):

            @pl.when(there)
            def _():
                halo_copy(step, group, side).start()

        inline_rows(half, rows - half)

    def cross_pass(step, group):
        for side, there in ((1, has_low), (0, has_high)):

            @pl.when(there)
            def _():
                halo_copy(step, group, side).wait_recv()

        @pl.loop(0, rows // PAIR)
        def _(trip):
            y = trip * PAIR
            accs = [[None] * 4 for _ in range(PAIR)]
            for line in range(taps + PAIR - 1):
                moved = [mid_buf[mid_at(step, group, y + line, comp), :] for comp in range(4)]
                for place in range(PAIR):
                    if 0 <= line - place < taps:
                        add_tap(accs[place], group, y + place, line - place, moved)
            for place, acc in enumerate(accs):
                for comp in range(4):
                    field_buf[field_at(group, comp, y + place), :] = acc[comp]
                term = acc[0] * acc[2] + acc[1] * acc[3]
                at = tile_rows(step * rows + y + place)
                if group == 0:
                    image_buf[at, :] = term
                else:
                    image_buf[at, :] = image_buf[at, :] + term

    for step in range(STEPS):
        for group in range(groups):
            inline_pass(step, group)
        for group in range(groups):
            cross_pass(step, group)

    for group in range(groups):
        for comp in range(4):
            for member in range(per_tile):
                for top in range(0, rows, SUBS):
                    for block in range(blocks):
                        start = ((group * 4 + comp) * rows + top) * SUBS + member * blocks + block
                        out_ref[
                            comp // 2, comp % 2, group * per_tile + member, top : top + SUBS,
                            block * LANES : (block + 1) * LANES,
                        ] = field_buf[pl.ds(start, SUBS, stride=SUBS), :]
    for step in range(STEPS):
        for top in range(0, rows, SUBS):
            for block in range(blocks):
                total = None
                for member in range(per_tile):
                    start = (step * rows + top) * SUBS + member * blocks + block
                    term = image_buf[pl.ds(start, SUBS, stride=SUBS), :]
                    total = term if total is None else total + term
                image_ref[step, top : top + SUBS, block * LANES : (block + 1) * LANES] = total

    for step in range(STEPS):
        for group in range(groups):
            for side, there in enumerate((has_low, has_high)):

                @pl.when(there)
                def _():
                    halo_copy(step, group, side).wait_send()


def on_device(strips, waves, levels, coeffs, angles, order):
    freqs, rows, cells = waves.shape[2:]
    level_count, taps = coeffs.shape[2:]
    blocks = cells // LANES
    per_tile = SUBS // blocks
    groups = freqs // per_tile
    assert blocks * per_tile == SUBS and groups * per_tile == freqs
    assert rows % SUBS == 0 and rows >= taps - 1 and level_count * taps <= LANES
    half = taps // 2
    sizes = (freqs, rows, blocks, per_tile, groups, level_count, taps, strips)
    tiles = lambda count: pltpu.VMEM((count * SUBS, LANES), jnp.float32)
    vmem, smem = pl.BlockSpec(memory_space=pltpu.VMEM), pl.BlockSpec(memory_space=pltpu.SMEM)
    return pl.pallas_call(
        functools.partial(kernel, sizes),
        out_shape=(
            jax.ShapeDtypeStruct(waves.shape, jnp.float32),
            jax.ShapeDtypeStruct((STEPS, rows, cells), jnp.float32),
        ),
        in_specs=[vmem, vmem, smem, smem, smem],
        out_specs=(vmem, vmem),
        scratch_shapes=[
            pltpu.VMEM((rows * SUBS, LANES), jnp.int32),
            tiles(groups * taps * 2 * level_count),
            tiles(groups * rows * taps * 2),
            tiles(groups * rows * 2),
            tiles(groups * 4 * rows),
            tiles(STEPS * groups * (rows + 2 * half) * 4),
            tiles(STEPS * rows),
            pltpu.SemaphoreType.DMA((STEPS, groups, 2)),
            pltpu.SemaphoreType.DMA((STEPS, groups, 2)),
        ],
        compiler_params=pltpu.CompilerParams(
            collective_id=0, has_side_effects=True, vmem_limit_bytes=48 * 1024 * 1024
        ),
    )(waves, levels, coeffs, angles, order)


def solution(mesh):
    in_specs = (P(None, None, "shot", "strip", None), P("strip", None), P(), P(), P("shot"))
    out_specs = (P(None, None, "shot", "strip", None), P("shot", "strip", None))
    return jax.shard_map(
        functools.partial(on_device, mesh.shape["strip"]),
        mesh=mesh,
        in_specs=in_specs,
        out_specs=out_specs,
        check_vma=False,
    )
```

```python
import functools

import jax
import jax.numpy as jnp
from jax import lax
from jax.experimental import pallas as pl
from jax.experimental.pallas import tpu as pltpu
from jax.sharding import PartitionSpec as P

STEPS = 2
LANES = 128
SUBS = 8
ROWS = 4
PAIR = 2
MESH = pl.DeviceIdType.MESH


def tile_rows(index, count=1):
    return pl.ds(pl.multiple_of(index * SUBS, SUBS), count * SUBS)


def kernel(
    sizes, waves_hbm, levels_hbm, coeffs_hbm, angles_ref, order_ref, out_ref, image_ref,
    waves_ref, levels_ref, coeffs_ref, load_sem,
    level_buf, table_buf, coef_buf, turn_buf, field_buf, mid_buf, image_buf, send_sem, recv_sem,
):
    freqs, rows, blocks, per_tile, groups, levels, taps, strips = sizes
    half = taps // 2
    span = rows + 2 * half
    me = lax.axis_index("strip")
    has_low, has_high = me > 0, me < strips - 1

    loads = [
        pltpu.make_async_copy(source, target, load_sem.at[i])
        for i, (source, target) in enumerate(
            ((coeffs_hbm, coeffs_ref), (levels_hbm, levels_ref), (waves_hbm, waves_ref))
        )
    ]
    for load in loads:
        load.start()

    def neighbour(step):
        return {"strip": me + step}

    barrier = pltpu.get_barrier_semaphore()
    for there, step in ((has_low, -1), (has_high, 1)):

        @pl.when(there)
        def _():
            pl.semaphore_signal(barrier, inc=1, device_id=neighbour(step), device_id_type=MESH)

    lane = lax.broadcasted_iota(jnp.int32, (SUBS, LANES), 1)
    sub = lax.broadcasted_iota(jnp.int32, (SUBS, LANES), 0)
    block_of = lax.rem(sub, blocks)

    loads[1].wait()
    for top in range(0, rows, SUBS):
        for block in range(blocks):
            cells = levels_ref[top : top + SUBS, block * LANES : (block + 1) * LANES]
            for member in range(per_tile):
                level_buf[pl.ds(top * SUBS + member * blocks + block, SUBS, stride=SUBS), :] = cells

    def table_at(group, tap, part, level):
        return tile_rows(((group * taps + tap) * 2 + part) * levels + level)

    def by_member(values):
        tile = jnp.full((SUBS, LANES), values[0], jnp.float32)
        for member in range(1, per_tile):
            tile = jnp.where(sub >= member * blocks, values[member], tile)
        return tile

    loads[0].wait()
    slots = [order_ref[f] for f in range(freqs)]
    turn_tabs = []
    for group in range(groups):
        members = slots[group * per_tile : (group + 1) * per_tile]
        turn = jnp.zeros((SUBS, LANES), jnp.float32)
        for level in range(levels):
            for tap in range(taps):
                for part in range(2):
                    table_buf[table_at(group, tap, part, level), :] = by_member(
                        [coeffs_ref[part, row, level, tap] for row in members]
                    )
            turn = jnp.where(lane == level, by_member([angles_ref[row, level] for row in members]), turn)
        for which, tab in enumerate((jnp.cos(turn), jnp.sin(turn))):
            turn_tabs.append([jnp.broadcast_to(tab[:, level : level + 1], (SUBS, LANES)) for level in range(levels)])

    def coef_at(group, y, tap, part):
        return tile_rows(((group * rows + y) * taps + tap) * 2 + part)

    def turn_at(group, y, which):
        return tile_rows((group * rows + y) * 2 + which)

    def choose(masks, entries):
        tile = entries[0]
        for mask, entry in zip(masks, entries[1:]):
            tile = jnp.where(mask, entry, tile)
        return tile

    @pl.loop(0, rows // PAIR)
    def _(trip):
        y = trip * PAIR
        masks = []
        for place in range(PAIR):
            level_tile = level_buf[tile_rows(y + place), :]
            masks.append([level_tile == level for level in range(1, levels)])
        for group in range(groups):
            for which in range(2):
                for place in range(PAIR):
                    turn_buf[turn_at(group, y + place, which), :] = choose(masks[place], turn_tabs[group * 2 + which])
            for tap in range(taps):
                for part in range(2):
                    entries = [table_buf[table_at(group, tap, part, level), :] for level in range(levels)]
                    for place in range(PAIR):
                        coef_buf[coef_at(group, y + place, tap, part), :] = choose(masks[place], entries)

    def field_at(group, comp, y):
        return tile_rows((group * 4 + comp) * rows + y)

    def mid_at(step, group, y, comp):
        return tile_rows(((step * groups + group) * span + y) * 4 + comp)

    loads[2].wait()
    for group in range(groups):
        for comp in range(4):
            for member in range(per_tile):
                for top in range(0, rows, SUBS):
                    for block in range(blocks):
                        cells = waves_ref[
                            comp // 2, comp % 2, group * per_tile + member, top : top + SUBS,
                            block * LANES : (block + 1) * LANES,
                        ]
                        start = ((group * 4 + comp) * rows + top) * SUBS + member * blocks + block
                        field_buf[pl.ds(start, SUBS, stride=SUBS), :] = cells

    for there, first in ((has_low, 0), (has_high, rows + half)):

        @pl.when(jnp.logical_not(there))
        def _():
            for step in range(STEPS):
                for group in range(groups):

                    @pl.loop(0, half * 4)
                    def _(i):
                        mid_buf[tile_rows(((step * groups + group) * span + first) * 4 + i), :] = jnp.zeros(
                            (SUBS, LANES), jnp.float32
                        )

    pl.semaphore_wait(barrier, has_low.astype(jnp.int32) + has_high.astype(jnp.int32))

    def halo_copy(step, group, side):
        source, target = ((half, rows + half), (rows, 0))[side]
        base = (step * groups + group) * span
        return pltpu.make_async_remote_copy(
            src_ref=mid_buf.at[tile_rows((base + source) * 4, half * 4)],
            dst_ref=mid_buf.at[tile_rows((base + target) * 4, half * 4)],
            send_sem=send_sem.at[step, group, side],
            recv_sem=recv_sem.at[step, group, side],
            device_id=neighbour((-1, 1)[side]),
            device_id_type=MESH,
        )

    def inline_row(step, group, y):
        cosine = turn_buf[turn_at(group, y, 0), :]
        sine = turn_buf[turn_at(group, y, 1), :]
        sr, si, rr, ri = [field_buf[field_at(group, comp, y), :] for comp in range(4)]
        cells = (sr * cosine - si * sine, sr * sine + si * cosine, rr * cosine + ri * sine, ri * cosine - rr * sine)
        before = [jnp.where(block_of == 0, 0.0, pltpu.roll(v, 1, 0)) for v in cells]
        after = [jnp.where(block_of == blocks - 1, 0.0, pltpu.roll(v, SUBS - 1, 0)) for v in cells]
        acc = [None] * 4
        for tap in range(taps):
            shift = tap - half
            if shift < 0:
                moved = [
                    pltpu.roll(jnp.where(lane < LANES + shift, v, w), -shift, 1) for v, w in zip(cells, before)
                ]
            elif shift > 0:
                moved = [
                    pltpu.roll(jnp.where(lane >= shift, v, w), LANES - shift, 1) for v, w in zip(cells, after)
                ]
            else:
                moved = cells
            add_tap(acc, group, y, tap, moved)
        for comp in range(4):
            mid_buf[mid_at(step, group, y + half, comp), :] = acc[comp]

    def add_tap(acc, group, y, tap, moved):
        cr = coef_buf[coef_at(group, y, tap, 0), :]
        ci = coef_buf[coef_at(group, y, tap, 1), :]
        sr, si, rr, ri = moved
        if acc[0] is None:
            acc[:] = [cr * sr - ci * si, cr * si + ci * sr, cr * rr + ci * ri, cr * ri - ci * rr]
        else:
            acc[0] = acc[0] + cr * sr - ci * si
            acc[1] = acc[1] + cr * si + ci * sr
            acc[2] = acc[2] + cr * rr + ci * ri
            acc[3] = acc[3] + cr * ri - ci * rr

    def trips(first, last, inline=None, cross=None):
        @pl.loop(first // ROWS, last // ROWS)
        def _(trip):
            for place in range(ROWS):
                if inline is not None:
                    inline_row(*inline, trip * ROWS + place)
                if cross is not None and place % PAIR == 0:
                    cross_rows(*cross, trip * ROWS + place)

    def send(step, group):
        for side, there in enumerate((has_low, has_high)):

            @pl.when(there)
            def _():
                halo_copy(step, group, side).start()

    def receive(step, group):
        for side, there in ((1, has_low), (0, has_high)):

            @pl.when(there)
            def _():
                halo_copy(step, group, side).wait_recv()

    def cross_rows(step, group, y):
        accs = [[None] * 4 for _ in range(PAIR)]
        for line in range(taps + PAIR - 1):
            moved = [mid_buf[mid_at(step, group, y + line, comp), :] for comp in range(4)]
            for place in range(PAIR):
                if 0 <= line - place < taps:
                    add_tap(accs[place], group, y + place, line - place, moved)
        for place, acc in enumerate(accs):
            for comp in range(4):
                field_buf[field_at(group, comp, y + place), :] = acc[comp]
            term = acc[0] * acc[2] + acc[1] * acc[3]
            at = tile_rows(step * rows + y + place)
            if group == 0:
                image_buf[at, :] = term
            else:
                image_buf[at, :] = image_buf[at, :] + term

    passes = [(step, group) for step in range(STEPS) for group in range(groups)]
    pending = []
    for step, group in passes:
        here = (step, group)
        beside = None
        if group == 0 and pending:
            while len(pending) > 1 or pending[0][1] == 0:
                before = pending.pop(0)
                receive(*before)
                trips(0, rows, cross=before)
            before = pending.pop(0)
            receive(*before)
            trips(0, half, here, before)
            trips(rows - half, rows, here, before)
            send(*here)
            trips(half, rows - half, here, before)
        else:
            trips(0, half, here)
            trips(rows - half, rows, here)
            send(*here)
            if pending:
                before = pending.pop(0)
                receive(*before)
                trips(half, rows - half, here, before)
                trips(0, half, cross=before)
                trips(rows - half, rows, cross=before)
            else:
                trips(half, rows - half, here)
        pending.append(here)
    for before in pending:
        receive(*before)
        trips(0, rows, cross=before)

    for group in range(groups):
        for comp in range(4):
            for member in range(per_tile):
                for top in range(0, rows, SUBS):
                    for block in range(blocks):
                        start = ((group * 4 + comp) * rows + top) * SUBS + member * blocks + block
                        out_ref[
                            comp // 2, comp % 2, group * per_tile + member, top : top + SUBS,
                            block * LANES : (block + 1) * LANES,
                        ] = field_buf[pl.ds(start, SUBS, stride=SUBS), :]
    for step in range(STEPS):
        for top in range(0, rows, SUBS):
            for block in range(blocks):
                total = None
                for member in range(per_tile):
                    start = (step * rows + top) * SUBS + member * blocks + block
                    term = image_buf[pl.ds(start, SUBS, stride=SUBS), :]
                    total = term if total is None else total + term
                image_ref[step, top : top + SUBS, block * LANES : (block + 1) * LANES] = total

    for step in range(STEPS):
        for group in range(groups):
            for side, there in enumerate((has_low, has_high)):

                @pl.when(there)
                def _():
                    halo_copy(step, group, side).wait_send()


def on_device(strips, waves, levels, coeffs, angles, order):
    freqs, rows, cells = waves.shape[2:]
    level_count, taps = coeffs.shape[2:]
    blocks = cells // LANES
    per_tile = SUBS // blocks
    groups = freqs // per_tile
    assert blocks * per_tile == SUBS and groups * per_tile == freqs
    assert rows % SUBS == 0 and rows >= taps - 1 and level_count * taps <= LANES
    half = taps // 2
    sizes = (freqs, rows, blocks, per_tile, groups, level_count, taps, strips)
    tiles = lambda count: pltpu.VMEM((count * SUBS, LANES), jnp.float32)
    vmem, smem, hbm = [pl.BlockSpec(memory_space=space) for space in (pltpu.VMEM, pltpu.SMEM, pltpu.HBM)]
    return pl.pallas_call(
        functools.partial(kernel, sizes),
        out_shape=(
            jax.ShapeDtypeStruct(waves.shape, jnp.float32),
            jax.ShapeDtypeStruct((STEPS, rows, cells), jnp.float32),
        ),
        in_specs=[hbm, hbm, hbm, smem, smem],
        out_specs=(vmem, vmem),
        scratch_shapes=[
            pltpu.VMEM(waves.shape, jnp.float32),
            pltpu.VMEM(levels.shape, jnp.int32),
            pltpu.SMEM(coeffs.shape, jnp.float32),
            pltpu.SemaphoreType.DMA((3,)),
            pltpu.VMEM((rows * SUBS, LANES), jnp.int32),
            tiles(groups * taps * 2 * level_count),
            tiles(groups * rows * taps * 2),
            tiles(groups * rows * 2),
            tiles(groups * 4 * rows),
            tiles(STEPS * groups * (rows + 2 * half) * 4),
            tiles(STEPS * rows),
            pltpu.SemaphoreType.DMA((STEPS, groups, 2)),
            pltpu.SemaphoreType.DMA((STEPS, groups, 2)),
        ],
        compiler_params=pltpu.CompilerParams(
            collective_id=0, has_side_effects=True, vmem_limit_bytes=67043328 - 1250000
        ),
    )(waves, levels, coeffs, angles, order)


def solution(mesh):
    in_specs = (P(None, None, "shot", "strip", None), P("strip", None), P(), P(), P("shot"))
    out_specs = (P(None, None, "shot", "strip", None), P("shot", "strip", None))
    return jax.shard_map(
        functools.partial(on_device, mesh.shape["strip"]),
        mesh=mesh,
        in_specs=in_specs,
        out_specs=out_specs,
        check_vma=False,
    )
```
